1024 devices in a mesh: grp: 4 (over z_hi), gy: 16 (over y, core), gz: 16 (over z_lo, x).
Axes of the slice: x: 8, y: 8, z: 8 (z_hi: 4, z_lo: 2; z = z_hi * 2 + z_lo), core: 2. Of those that a mesh axis runs over, the one named last changes fastest.
Arguments:
- velocity: float32 [3, 128, 128, 512], P(None, 'gy', 'gz', 'grp'), may hold values from -5 to 5
- basis_old: bfloat16 [64, 3, 64, 64, 512], P(None, None, 'gy', 'gz', 'grp'), may hold values from -64 to 64
- strength: float32 [64], replicated, may hold values from 0.3 to 3
- snapshots: bfloat16 [63, 3, 64, 64, 512], P(None, None, 'gy', 'gz', 'grp'), may hold values from -64 to 64
Outputs:
- advanced: float32 [3, 128, 128, 512], P(None, 'gy', 'gz', 'grp')
- basis_new: bfloat16 [128, 3, 64, 64, 512], P(None, None, 'gy', 'gz', 'grp')
- root_factor: float32 [128, 128], replicated
The draws below stay inside these ranges and needn't reach their ends.
All inputs are finite; a program needn't handle non-finite values.
Results may differ from the reference program's by a relative error of at most 0.0012.
The reference program's roundings to bfloat16 on the way (of `newest`, `head`, `whole` and `weights`) count: a program that leaves them out, or rounds other values in their place, can miss the bound.
Values sent between devices are 32-bit elements; how exact they have to be, the bound alone decides.
No kernel may reach another device: no remote copies, remote signals or barrier semaphores. Data moves between devices by JAX's collectives and lax.ppermute only.
A program may use at most 32 MiB of HBM per device.

```python
import math
import jax
import jax.numpy as jnp
from jax import lax

MODES = 64
BATCH = 63
NS_ITERS = 8
NX = 512
NY = 128
NZ = 128
RANKS = 128
MROWS = 6291456


def shared_fields(key):
    return jax.random.normal(jax.random.fold_in(key, 9001), (4, 3, NY // 2, NZ // 2, NX), jnp.float32)


def mixed_rows(key, row_count, salt_value):
    fields = shared_fields(key)
    salted = jax.random.fold_in(key, salt_value)
    leading = jax.random.uniform(jax.random.fold_in(salted, 1), (row_count, 1), jnp.float32, 0.5, 1.0)
    others = 0.5 * jax.random.normal(jax.random.fold_in(salted, 2), (row_count, 3), jnp.float32)
    coeffs = jnp.concatenate([leading, others], axis=1)
    fluctuation = jax.random.normal(jax.random.fold_in(salted, 3), (row_count, 3, NY // 2, NZ // 2, NX), jnp.float32)
    return jnp.einsum('rk,kcyzx->rcyzx', coeffs, fields) + fluctuation


def scaled_rows(key, row_count, salt_value):
    rows = mixed_rows(key, row_count, salt_value)
    return jnp.clip(rows, -64.0, 64.0).astype(jnp.bfloat16)


def draw_basis_old(key, part):
    return scaled_rows(key, MODES, 11)


def draw_snapshots(key, part):
    return scaled_rows(key, BATCH, 21)


def draw_velocity(key, part):
    leading = shared_fields(key)[0]
    magnitude = jax.random.uniform(jax.random.fold_in(key, 31), (3, NY, NZ, NX), jnp.float32, 2.0, 5.0)
    coin = jax.random.uniform(jax.random.fold_in(key, 32), (3, NY, NZ, NX), jnp.float32)
    signed = jnp.where(coin < 0.5, -magnitude, magnitude)
    placed = jnp.zeros((3, NY, NZ, NX), jnp.float32).at[:, ::2, ::2, :].set(0.6 * leading)
    return jnp.clip(signed + placed, -5.0, 5.0)


def setup_inputs(seed: int = 0) -> dict:
    streams_of = jax.random.split(jax.random.key(seed), 5)
    velocity = draw_velocity(jax.random.fold_in(streams_of[4], 71), 0)
    basis_old = draw_basis_old(jax.random.fold_in(streams_of[4], 71), 0)
    strength = jnp.clip(jnp.exp(jax.random.uniform(streams_of[2], (MODES,), jnp.float32, math.log(0.3), math.log(3.0))), 0.3, 3.0)
    snapshots = draw_snapshots(jax.random.fold_in(streams_of[4], 71), 0)
    return {"velocity": velocity, "basis_old": basis_old, "strength": strength, "snapshots": snapshots}


time_step = 0.1
viscosity = 0.05

def padding(field):
    wrapped = jnp.pad(field, ((0, 0), (0, 0), (1, 1), (1, 1)), mode='wrap')
    return jnp.pad(wrapped, ((0, 0), (1, 1), (0, 0), (0, 0)))

def tendency(padded, field):
    y_plus = padded[:, 2:, 1:-1, 1:-1]
    y_minus = padded[:, :-2, 1:-1, 1:-1]
    z_plus = padded[:, 1:-1, 2:, 1:-1]
    z_minus = padded[:, 1:-1, :-2, 1:-1]
    x_plus = padded[:, 1:-1, 1:-1, 2:]
    x_minus = padded[:, 1:-1, 1:-1, :-2]
    carried = field[0][None] * (x_plus - x_minus) * 0.5
    carried = carried + field[1][None] * (y_plus - y_minus) * 0.5
    carried = carried + field[2][None] * (z_plus - z_minus) * 0.5
    spread = x_plus + x_minus + y_plus + y_minus + z_plus + z_minus - 6.0 * field
    return viscosity * spread - carried

def reference(velocity, basis_old, strength, snapshots):
    field = velocity
    for repeat in range(2):
        first = field + time_step * tendency(padding(field), field)
        second = 0.75 * field + 0.25 * (first + time_step * tendency(padding(first), first))
        field = field / 3.0 + 2.0 / 3.0 * (second + time_step * tendency(padding(second), second))
    newest = field[:, ::2, ::2, :].reshape(1, -1).astype(jnp.bfloat16)
    head = (strength[:, None] * basis_old.reshape(MODES, -1).astype(jnp.float32)).astype(jnp.bfloat16)
    whole = jnp.concatenate([head, snapshots.reshape(BATCH, -1), newest], axis=0)
    gram = jnp.dot(whole, whole.T, preferred_element_type=jnp.float32)
    scale = jnp.sqrt(jnp.sum(gram * gram))
    level = gram / scale
    ident = jnp.eye(RANKS, dtype=jnp.float32)
    inverse = ident
    for repeat in range(NS_ITERS):
        factor = 1.5 * ident - 0.5 * jnp.dot(inverse, level, precision=lax.Precision.HIGHEST)
        level = jnp.dot(level, factor, precision=lax.Precision.HIGHEST)
        inverse = jnp.dot(factor, inverse, precision=lax.Precision.HIGHEST)
    weights = (inverse * (jnp.sqrt(jnp.float32(MROWS)) / jnp.sqrt(scale))).astype(jnp.bfloat16)
    block_count = 3 * (NY // 2)
    whole_blocks = whole.reshape(RANKS, block_count, -1)

    def rotate(block_index):
        block = lax.dynamic_index_in_dim(whole_blocks, block_index, 1, keepdims=False)
        return jnp.dot(weights, block, preferred_element_type=jnp.float32).astype(jnp.bfloat16)
    pieces = lax.map(rotate, jnp.arange(block_count, dtype=jnp.int32))
    basis_new = jnp.transpose(pieces, (1, 0, 2)).reshape(RANKS, 3, NY // 2, NZ // 2, NX)
    return (field, basis_new, level)
```

```python
import functools
import jax
import jax.numpy as jnp
from jax import lax
from jax.experimental import pallas as pl
from jax.experimental.pallas import tpu as pltpu
from jax.sharding import PartitionSpec as P

NS_ITERS = 8

HALO = 6
PLANES = 20
DT = 0.1
VISC = 0.05


def _lanes():
    return lax.broadcasted_iota(jnp.int32, (8, 128), 1)


def _faces_y_kernel(v_ref, zl_ref, zh_ref, low_ref, high_ref):
    for part, source in enumerate((zl_ref, v_ref, zh_ref)):
        rows = pl.ds(8 * part, 8)
        low_ref[:, :, rows, :] = source[:, 0:HALO]
        high_ref[:, :, rows, :] = source[:, 8 - HALO : 8]


def _plane(part, c, k, v_refs, yl_ref, yh_ref):
    rows = pl.ds(8 * part, 8)
    if k < HALO:
        return yl_ref[c, k, rows, :]
    if k < HALO + 8:
        return v_refs[part][c, k - HALO]
    return yh_ref[c, k - HALO - 8, rows, :]


def _faces_x_kernel(v_ref, zl_ref, zh_ref, yl_ref, yh_ref, low_ref, high_ref):
    lane = _lanes()
    sources = (zl_ref, v_ref, zh_ref)
    for c in range(3):
        for part in range(3):
            low = high = None
            for k in range(PLANES):
                tile = _plane(part, c, k, sources, yl_ref, yh_ref)
                first = pltpu.roll(tile, (HALO * k) % 128, 1)
                last = pltpu.roll(tile, (HALO * k + HALO) % 128, 1)
                if k == 0:
                    low, high = first, last
                else:
                    keep = lane < HALO * k
                    low = jnp.where(keep, low, first)
                    high = jnp.where(keep, high, last)
            low_ref[3 * c + part] = low
            high_ref[3 * c + part] = high


def _rotated(tiles, lane):
    up = [pltpu.roll(t, 127, 1) for t in tiles]
    down = [pltpu.roll(t, 1, 1) for t in tiles]
    plus = [jnp.where(lane == 127, up[1 - i], up[i]) for i in range(2)]
    minus = [jnp.where(lane == 0, down[1 - i], down[i]) for i in range(2)]
    return plus, minus


def _euler(u_ref, y, row, tiles):
    lane = _lanes()
    u = [[u_ref[c, y, t, row : row + 8, :] for t in range(2)] for c in range(3)]
    half = [[u[c][t] * (0.5 * DT) for t in range(tiles)] for c in range(3)]
    out = []
    for c in range(3):
        plus, minus = _rotated(u[c], lane)
        outs = []
        for t in range(tiles):
            yp = u_ref[c, y + 1, t, row : row + 8, :]
            ym = u_ref[c, y - 1, t, row : row + 8, :]
            zp = u_ref[c, y, t, row + 1 : row + 9, :]
            zm = u_ref[c, y, t, row - 1 : row + 7, :]
            carried = (
                half[0][t] * (plus[t] - minus[t])
                + half[1][t] * (yp - ym)
                + half[2][t] * (zp - zm)
            )
            around = (plus[t] + minus[t]) + (yp + ym) + (zp + zm)
            outs.append(u[c][t] + ((DT * VISC) * (around - 6.0 * u[c][t]) - carried))
        out.append(outs)
    return out


def _stencil_kernel(
    gy_ref, v_ref, zl_ref, zh_ref, yl_ref, yh_ref, xh_ref, xl_ref, adv_ref, new_ref, a_ref, b_ref, c_ref, *, last
):
    lane = _lanes()
    sources = (zl_ref, v_ref, zh_ref)
    for part in range(3):
        rows = pl.ds(8 + 8 * part, 8)
        a_ref[:, HALO : HALO + 8, 0, rows, :] = sources[part][...]
        a_ref[:, 0:HALO, 0, rows, :] = yl_ref[:, :, pl.ds(8 * part, 8), :]
        a_ref[:, HALO + 8 : PLANES, 0, rows, :] = yh_ref[:, :, pl.ds(8 * part, 8), :]
        for c in range(3):
            right = xh_ref[3 * c + part]
            left = xl_ref[3 * c + part]
            for k in range(PLANES):
                a_ref[c, k, 1, rows, :] = jnp.where(
                    lane < 64,
                    pltpu.roll(right, (-HALO * k) % 128, 1),
                    pltpu.roll(left, (128 - HALO - HALO * k) % 128, 1),
                )

    gy = gy_ref[0]

    def close(ref):
        @pl.when(gy == 0)
        def _():
            ref[:, HALO - 1] = jnp.zeros((3, 2, 40, 128), jnp.float32)

        @pl.when(gy == last)
        def _():
            ref[:, HALO + 8] = jnp.zeros((3, 2, 40, 128), jnp.float32)

    def stage(source, target, combine, depth):
        @pl.loop(depth, PLANES - depth)
        def _(y):
            for row in (8, 16, 24):
                moved = _euler(source, y, row, 2)
                for c in range(3):
                    for t in range(2):
                        target[c, y, t, row : row + 8, :] = combine(moved[c][t], c, y, t, row)

        close(target)

    def keep(w, c, y, t, row):
        return w

    def quarter(w, c, y, t, row):
        return 0.75 * a_ref[c, y, t, row : row + 8, :] + 0.25 * w

    def third(w, c, y, t, row):
        return a_ref[c, y, t, row : row + 8, :] * (1.0 / 3.0) + (2.0 / 3.0) * w

    close(a_ref)
    stage(a_ref, b_ref, keep, 1)
    stage(b_ref, c_ref, quarter, 2)
    stage(c_ref, a_ref, third, 3)
    stage(a_ref, b_ref, keep, 4)
    stage(b_ref, c_ref, quarter, 5)
    for y in range(HALO, HALO + 8):
        moved = _euler(c_ref, y, 16, 1)
        for c in range(3):
            adv_ref[c, y - HALO] = third(moved[c][0], c, y, 0, 16)
    for c in range(3):
        for y in range(0, 8, 2):
            new_ref[c, y // 2] = adv_ref[c, y, pl.ds(0, 4, stride=2), :]


VMEM_SPEC = pl.BlockSpec(memory_space=pltpu.VMEM)
SMEM_SPEC = pl.BlockSpec(memory_space=pltpu.SMEM)


def shift(x, axis, step):
    n = lax.axis_size(axis)
    return lax.ppermute(x, axis, [(i, (i + step) % n) for i in range(n)])


def advance(v):
    f32 = jnp.float32
    zl = shift(v, "gz", 1)
    zh = shift(v, "gz", -1)
    low, high = pl.pallas_call(
        _faces_y_kernel,
        out_shape=[jax.ShapeDtypeStruct((3, HALO, 24, 128), f32)] * 2,
        in_specs=[VMEM_SPEC] * 3,
        out_specs=[VMEM_SPEC] * 2,
        name="faces_y",
    )(v, zl, zh)
    yl = shift(high, "gy", 1)
    yh = shift(low, "gy", -1)
    low, high = pl.pallas_call(
        _faces_x_kernel,
        out_shape=[jax.ShapeDtypeStruct((9, 8, 128), f32)] * 2,
        in_specs=[VMEM_SPEC] * 5,
        out_specs=[VMEM_SPEC] * 2,
        name="faces_x",
    )(v, zl, zh, yl, yh)
    xl = shift(high, "grp", 1)
    xh = shift(low, "grp", -1)
    gy = lax.axis_index("gy").astype(jnp.int32).reshape(1)
    return pl.pallas_call(
        functools.partial(_stencil_kernel, last=lax.axis_size("gy") - 1),
        out_shape=[jax.ShapeDtypeStruct((3, 8, 8, 128), f32), jax.ShapeDtypeStruct((3, 4, 4, 128), f32)],
        in_specs=[SMEM_SPEC] + [VMEM_SPEC] * 7,
        out_specs=[VMEM_SPEC] * 2,
        scratch_shapes=[pltpu.VMEM((3, PLANES, 2, 40, 128), f32)] * 3,
        name="stencil",
    )(gy, v, zl, zh, yl, yh, xh, xl)


def _pack_kernel(g_ref, out_ref):
    row = lax.broadcasted_iota(jnp.int32, (64, 128), 0)
    lane = lax.broadcasted_iota(jnp.int32, (64, 128), 1)
    top = g_ref[0:64, :]
    bottom = g_ref[64:128, :]
    out_ref[0:64, :] = jnp.where(lane < row, pltpu.roll(bottom, 64, 1), top)
    diagonal = jnp.where(lane == row + 64, bottom, 0.0)
    out_ref[64:72, :] = jnp.broadcast_to(jnp.sum(diagonal, axis=0, keepdims=True), (8, 128))


def _unpacked(packed):
    row = lax.broadcasted_iota(jnp.int32, (64, 128), 0)
    lane = lax.broadcasted_iota(jnp.int32, (64, 128), 1)
    top = packed[0:64]
    diagonal = packed[64:65]
    turned = jnp.concatenate([top, top], axis=0).T
    upper_left = turned[0:64]
    bottom_left = turned[64:128]
    top_full = jnp.where(lane < row, upper_left, top)
    moved = pltpu.roll(top, 64, 1)
    bottom = jnp.where(lane > row + 64, upper_left, moved)
    bottom = jnp.where(lane == row + 64, diagonal, bottom)
    bottom = jnp.where(lane < 64, bottom_left, bottom)
    return jnp.concatenate([top_full, bottom], axis=0)


def _iterate_kernel(packed_ref, level_ref, weights_ref, *, total_rows):
    gram = _unpacked(packed_ref[...])
    scale = jnp.sqrt(jnp.sum(gram * gram, keepdims=True))
    level = gram / scale
    ident = (
        lax.broadcasted_iota(jnp.int32, (128, 128), 0) == lax.broadcasted_iota(jnp.int32, (128, 128), 1)
    ).astype(jnp.float32)

    def dot(a, b):
        return jnp.dot(a, b, precision=lax.Precision.HIGHEST, preferred_element_type=jnp.float32)

    inverse = ident
    for repeat in range(NS_ITERS):
        product = dot(inverse, level) if repeat else level
        factor = 1.5 * ident - 0.5 * product
        level = dot(level, factor)
        inverse = dot(factor, inverse) if repeat else factor
    level_ref[...] = level
    ratio = jnp.sqrt(jnp.float32(total_rows)) / jnp.sqrt(scale)
    weights_ref[...] = (inverse * ratio).astype(jnp.bfloat16)


def local(velocity, basis_old, strength, snapshots):
    modes = basis_old.shape[0]
    earlier_count = snapshots.shape[0]
    ranks = modes + earlier_count + 1
    head = (strength[:, None] * basis_old.reshape(modes, -1).astype(jnp.float32)).astype(jnp.bfloat16)
    field, newest = advance(velocity)
    newest = newest.reshape(1, -1).astype(jnp.bfloat16)
    whole = jnp.concatenate([head, snapshots.reshape(earlier_count, -1), newest], axis=0)
    gram = jnp.dot(whole, whole.T, preferred_element_type=jnp.float32)
    packed = pl.pallas_call(
        _pack_kernel,
        out_shape=jax.ShapeDtypeStruct((72, 128), jnp.float32),
        in_specs=[VMEM_SPEC],
        out_specs=VMEM_SPEC,
        name="pack",
    )(gram)
    packed = lax.psum(packed, ("grp", "gy", "gz"))
    total_rows = whole.shape[1] * lax.axis_size("grp") * lax.axis_size("gy") * lax.axis_size("gz")
    level, weights = pl.pallas_call(
        functools.partial(_iterate_kernel, total_rows=total_rows),
        out_shape=[
            jax.ShapeDtypeStruct((ranks, ranks), jnp.float32),
            jax.ShapeDtypeStruct((ranks, ranks), jnp.bfloat16),
        ],
        in_specs=[VMEM_SPEC],
        out_specs=[VMEM_SPEC] * 2,
        name="iterate",
    )(packed)
    basis_new = jnp.dot(weights, whole, preferred_element_type=jnp.float32).astype(jnp.bfloat16)
    basis_new = basis_new.reshape(ranks, 3, field.shape[1] // 2, field.shape[2] // 2, field.shape[3])
    return (field, basis_new, level)


def solution(mesh):
    placed = (
        P(None, "gy", "gz", "grp"),
        P(None, None, "gy", "gz", "grp"),
        P(),
        P(None, None, "gy", "gz", "grp"),
    )
    return jax.shard_map(
        local,
        mesh=mesh,
        in_specs=placed,
        out_specs=(P(None, "gy", "gz", "grp"), P(None, None, "gy", "gz", "grp"), P()),
        check_vma=False,
    )
```

```python
import functools
import jax
import jax.numpy as jnp
from jax import lax
from jax.experimental import pallas as pl
from jax.experimental.pallas import tpu as pltpu
from jax.sharding import PartitionSpec as P

NS_ITERS = 8

HALO = 6
PLANES = 20
DT = 0.1
VISC = 0.05


def _lanes():
    return lax.broadcasted_iota(jnp.int32, (8, 128), 1)


def _faces_y_kernel(v_ref, zl_ref, zh_ref, low_ref, high_ref):
    for part, source in enumerate((zl_ref, v_ref, zh_ref)):
        rows = pl.ds(8 * part, 8)
        low_ref[:, :, rows, :] = source[:, 0:HALO]
        high_ref[:, :, rows, :] = source[:, 8 - HALO : 8]


def _plane(part, c, k, v_refs, yl_ref, yh_ref):
    rows = pl.ds(8 * part, 8)
    if k < HALO:
        return yl_ref[c, k, rows, :]
    if k < HALO + 8:
        return v_refs[part][c, k - HALO]
    return yh_ref[c, k - HALO - 8, rows, :]


def _faces_x_kernel(v_ref, zl_ref, zh_ref, yl_ref, yh_ref, low_ref, high_ref):
    lane = _lanes()
    sources = (zl_ref, v_ref, zh_ref)
    for c in range(3):
        for part in range(3):
            low = high = None
            for k in range(PLANES):
                tile = _plane(part, c, k, sources, yl_ref, yh_ref)
                first = pltpu.roll(tile, (HALO * k) % 128, 1)
                last = pltpu.roll(tile, (HALO * k + HALO) % 128, 1)
                if k == 0:
                    low, high = first, last
                else:
                    keep = lane < HALO * k
                    low = jnp.where(keep, low, first)
                    high = jnp.where(keep, high, last)
            low_ref[3 * c + part] = low
            high_ref[3 * c + part] = high


def _rotated(tiles, lane):
    up = [pltpu.roll(t, 127, 1) for t in tiles]
    down = [pltpu.roll(t, 1, 1) for t in tiles]
    plus = [jnp.where(lane == 127, up[1 - i], up[i]) for i in range(2)]
    minus = [jnp.where(lane == 0, down[1 - i], down[i]) for i in range(2)]
    return plus, minus


def _euler(u_ref, y, row, tiles):
    lane = _lanes()
    u = [[u_ref[c, y, t, row : row + 8, :] for t in range(2)] for c in range(3)]
    half = [[u[c][t] * (0.5 * DT) for t in range(tiles)] for c in range(3)]
    out = []
    for c in range(3):
        plus, minus = _rotated(u[c], lane)
        outs = []
        for t in range(tiles):
            yp = u_ref[c, y + 1, t, row : row + 8, :]
            ym = u_ref[c, y - 1, t, row : row + 8, :]
            zp = u_ref[c, y, t, row + 1 : row + 9, :]
            zm = u_ref[c, y, t, row - 1 : row + 7, :]
            carried = (
                half[0][t] * (plus[t] - minus[t])
                + half[1][t] * (yp - ym)
                + half[2][t] * (zp - zm)
            )
            around = (plus[t] + minus[t]) + (yp + ym) + (zp + zm)
            outs.append(u[c][t] + ((DT * VISC) * (around - 6.0 * u[c][t]) - carried))
        out.append(outs)
    return out


def _stencil_kernel(
    gy_ref, v_ref, zl_ref, zh_ref, yl_ref, yh_ref, xh_ref, xl_ref, adv_ref, new_ref, a_ref, b_ref, c_ref, *, last
):
    lane = _lanes()
    sources = (zl_ref, v_ref, zh_ref)
    for part in range(3):
        rows = pl.ds(8 + 8 * part, 8)
        a_ref[:, HALO : HALO + 8, 0, rows, :] = sources[part][...]
        a_ref[:, 0:HALO, 0, rows, :] = yl_ref[:, :, pl.ds(8 * part, 8), :]
        a_ref[:, HALO + 8 : PLANES, 0, rows, :] = yh_ref[:, :, pl.ds(8 * part, 8), :]
        for c in range(3):
            right = xh_ref[3 * c + part]
            left = xl_ref[3 * c + part]
            for k in range(PLANES):
                a_ref[c, k, 1, rows, :] = jnp.where(
                    lane < 64,
                    pltpu.roll(right, (-HALO * k) % 128, 1),
                    pltpu.roll(left, (128 - HALO - HALO * k) % 128, 1),
                )

    gy = gy_ref[0]

    def close(ref):
        @pl.when(gy == 0)
        def _():
            ref[:, HALO - 1] = jnp.zeros((3, 2, 40, 128), jnp.float32)

        @pl.when(gy == last)
        def _():
            ref[:, HALO + 8] = jnp.zeros((3, 2, 40, 128), jnp.float32)

    def stage(source, target, combine, depth):
        @pl.loop(depth, PLANES - depth)
        def _(y):
            for row in (8, 16, 24):
                moved = _euler(source, y, row, 2)
                for c in range(3):
                    for t in range(2):
                        target[c, y, t, row : row + 8, :] = combine(moved[c][t], c, y, t, row)

        close(target)

    def keep(w, c, y, t, row):
        return w

    def quarter(w, c, y, t, row):
        return 0.75 * a_ref[c, y, t, row : row + 8, :] + 0.25 * w

    def third(w, c, y, t, row):
        return a_ref[c, y, t, row : row + 8, :] * (1.0 / 3.0) + (2.0 / 3.0) * w

    close(a_ref)
    stage(a_ref, b_ref, keep, 1)
    stage(b_ref, c_ref, quarter, 2)
    stage(c_ref, a_ref, third, 3)
    stage(a_ref, b_ref, keep, 4)
    stage(b_ref, c_ref, quarter, 5)
    for y in range(HALO, HALO + 8):
        moved = _euler(c_ref, y, 16, 1)
        for c in range(3):
            adv_ref[c, y - HALO] = third(moved[c][0], c, y, 0, 16)
    for c in range(3):
        for y in range(0, 8, 2):
            new_ref[c, y // 2] = adv_ref[c, y, pl.ds(0, 4, stride=2), :]


VMEM_SPEC = pl.BlockSpec(memory_space=pltpu.VMEM)
SMEM_SPEC = pl.BlockSpec(memory_space=pltpu.SMEM)


def shift(x, axis, step):
    n = lax.axis_size(axis)
    return lax.ppermute(x, axis, [(i, (i + step) % n) for i in range(n)])


def advance(v):
    f32 = jnp.float32
    zl = shift(v, "gz", 1)
    zh = shift(v, "gz", -1)
    low, high = pl.pallas_call(
        _faces_y_kernel,
        out_shape=[jax.ShapeDtypeStruct((3, HALO, 24, 128), f32)] * 2,
        in_specs=[VMEM_SPEC] * 3,
        out_specs=[VMEM_SPEC] * 2,
        name="faces_y",
    )(v, zl, zh)
    yl = shift(high, "gy", 1)
    yh = shift(low, "gy", -1)
    low, high = pl.pallas_call(
        _faces_x_kernel,
        out_shape=[jax.ShapeDtypeStruct((9, 8, 128), f32)] * 2,
        in_specs=[VMEM_SPEC] * 5,
        out_specs=[VMEM_SPEC] * 2,
        name="faces_x",
    )(v, zl, zh, yl, yh)
    xl = shift(high, "grp", 1)
    xh = shift(low, "grp", -1)
    gy = lax.axis_index("gy").astype(jnp.int32).reshape(1)
    return pl.pallas_call(
        functools.partial(_stencil_kernel, last=lax.axis_size("gy") - 1),
        out_shape=[jax.ShapeDtypeStruct((3, 8, 8, 128), f32), jax.ShapeDtypeStruct((3, 4, 4, 128), f32)],
        in_specs=[SMEM_SPEC] + [VMEM_SPEC] * 7,
        out_specs=[VMEM_SPEC] * 2,
        scratch_shapes=[pltpu.VMEM((3, PLANES, 2, 40, 128), f32)] * 3,
        name="stencil",
    )(gy, v, zl, zh, yl, yh, xh, xl)


def exchanged(blocks, axes):
    return lax.all_to_all(blocks, axes, 0, 0)


def summed(gram):
    lanes = gram.shape[1]
    parts = lax.axis_size("gz")
    rows = gram.shape[0] // parts
    others = lax.axis_size("grp") * lax.axis_size("gy")
    mine = jnp.sum(exchanged(gram.reshape(parts, rows, lanes), "gz"), axis=0)
    mine = jnp.sum(exchanged(jnp.broadcast_to(mine[None], (others, rows, lanes)), ("grp", "gy")), axis=0)
    return exchanged(jnp.broadcast_to(mine[None], (parts, rows, lanes)), "gz").reshape(gram.shape)


def _iterate_kernel(gram_ref, level_ref, weights_ref, *, total_rows):
    gram = gram_ref[...]
    scale = jnp.sqrt(jnp.sum(gram * gram, keepdims=True))
    level = gram / scale
    ident = (
        lax.broadcasted_iota(jnp.int32, (128, 128), 0) == lax.broadcasted_iota(jnp.int32, (128, 128), 1)
    ).astype(jnp.float32)

    def dot(a, b):
        return jnp.dot(a, b, precision=lax.Precision.HIGHEST, preferred_element_type=jnp.float32)

    inverse = ident
    for repeat in range(NS_ITERS):
        product = dot(inverse, level) if repeat else level
        factor = 1.5 * ident - 0.5 * product
        level = dot(level, factor)
        inverse = dot(factor, inverse) if repeat else factor
    level_ref[...] = level
    ratio = jnp.sqrt(jnp.float32(total_rows)) / jnp.sqrt(scale)
    weights_ref[...] = (inverse * ratio).astype(jnp.bfloat16)


def local(velocity, basis_old, strength, snapshots):
    modes = basis_old.shape[0]
    earlier_count = snapshots.shape[0]
    ranks = modes + earlier_count + 1
    head = (strength[:, None] * basis_old.reshape(modes, -1).astype(jnp.float32)).astype(jnp.bfloat16)
    field, newest = advance(velocity)
    newest = newest.reshape(1, -1).astype(jnp.bfloat16)
    whole = jnp.concatenate([head, snapshots.reshape(earlier_count, -1), newest], axis=0)
    gram = jnp.dot(whole, whole.T, preferred_element_type=jnp.float32)
    gram = summed(gram)
    total_rows = whole.shape[1] * lax.axis_size("grp") * lax.axis_size("gy") * lax.axis_size("gz")
    level, weights = pl.pallas_call(
        functools.partial(_iterate_kernel, total_rows=total_rows),
        out_shape=[
            jax.ShapeDtypeStruct((ranks, ranks), jnp.float32),
            jax.ShapeDtypeStruct((ranks, ranks), jnp.bfloat16),
        ],
        in_specs=[VMEM_SPEC],
        out_specs=[VMEM_SPEC] * 2,
        name="iterate",
    )(gram)
    basis_new = jnp.dot(weights, whole, preferred_element_type=jnp.float32).astype(jnp.bfloat16)
    basis_new = basis_new.reshape(ranks, 3, field.shape[1] // 2, field.shape[2] // 2, field.shape[3])
    return (field, basis_new, level)


def solution(mesh):
    placed = (
        P(None, "gy", "gz", "grp"),
        P(None, None, "gy", "gz", "grp"),
        P(),
        P(None, None, "gy", "gz", "grp"),
    )
    return jax.shard_map(
        local,
        mesh=mesh,
        in_specs=placed,
        out_specs=(P(None, "gy", "gz", "grp"), P(None, None, "gy", "gz", "grp"), P()),
        check_vma=False,
    )
```

```python
import functools
import jax
import jax.numpy as jnp
from jax import lax
from jax.experimental import pallas as pl
from jax.experimental.pallas import tpu as pltpu
from jax.sharding import PartitionSpec as P

NS_ITERS = 8

HALO = 6
PLANES = 20
DT = 0.1
VISC = 0.05


def _lanes():
    return lax.broadcasted_iota(jnp.int32, (8, 128), 1)


def _faces_y_kernel(v_ref, zl_ref, zh_ref, low_ref, high_ref):
    for part, source in enumerate((zl_ref, v_ref, zh_ref)):
        rows = pl.ds(8 * part, 8)
        low_ref[:, :, rows, :] = source[:, 0:HALO]
        high_ref[:, :, rows, :] = source[:, 8 - HALO : 8]


def _plane(part, c, k, v_refs, yl_ref, yh_ref):
    rows = pl.ds(8 * part, 8)
    if k < HALO:
        return yl_ref[c, k, rows, :]
    if k < HALO + 8:
        return v_refs[part][c, k - HALO]
    return yh_ref[c, k - HALO - 8, rows, :]


def _faces_x_kernel(v_ref, zl_ref, zh_ref, yl_ref, yh_ref, low_ref, high_ref):
    lane = _lanes()
    sources = (zl_ref, v_ref, zh_ref)
    for c in range(3):
        for part in range(3):
            low = high = None
            for k in range(PLANES):
                tile = _plane(part, c, k, sources, yl_ref, yh_ref)
                first = pltpu.roll(tile, (HALO * k) % 128, 1)
                last = pltpu.roll(tile, (HALO * k + HALO) % 128, 1)
                if k == 0:
                    low, high = first, last
                else:
                    keep = lane < HALO * k
                    low = jnp.where(keep, low, first)
                    high = jnp.where(keep, high, last)
            low_ref[3 * c + part] = low
            high_ref[3 * c + part] = high


def _rotated(tiles, lane):
    up = [pltpu.roll(t, 127, 1) for t in tiles]
    down = [pltpu.roll(t, 1, 1) for t in tiles]
    plus = [jnp.where(lane == 127, up[1 - i], up[i]) for i in range(2)]
    minus = [jnp.where(lane == 0, down[1 - i], down[i]) for i in range(2)]
    return plus, minus


def _euler(u_ref, y, row, tiles):
    lane = _lanes()
    u = [[u_ref[c, y, t, row : row + 8, :] for t in range(2)] for c in range(3)]
    half = [[u[c][t] * (0.5 * DT) for t in range(tiles)] for c in range(3)]
    out = []
    for c in range(3):
        plus, minus = _rotated(u[c], lane)
        outs = []
        for t in range(tiles):
            yp = u_ref[c, y + 1, t, row : row + 8, :]
            ym = u_ref[c, y - 1, t, row : row + 8, :]
            zp = u_ref[c, y, t, row + 1 : row + 9, :]
            zm = u_ref[c, y, t, row - 1 : row + 7, :]
            carried = (
                half[0][t] * (plus[t] - minus[t])
                + half[1][t] * (yp - ym)
                + half[2][t] * (zp - zm)
            )
            around = (plus[t] + minus[t]) + (yp + ym) + (zp + zm)
            outs.append(u[c][t] + ((DT * VISC) * (around - 6.0 * u[c][t]) - carried))
        out.append(outs)
    return out


def _stencil_kernel(
    gy_ref, v_ref, zl_ref, zh_ref, yl_ref, yh_ref, xh_ref, xl_ref, adv_ref, new_ref, a_ref, b_ref, c_ref, *, last
):
    lane = _lanes()
    sources = (zl_ref, v_ref, zh_ref)
    for part in range(3):
        rows = pl.ds(8 + 8 * part, 8)
        a_ref[:, HALO : HALO + 8, 0, rows, :] = sources[part][...]
        a_ref[:, 0:HALO, 0, rows, :] = yl_ref[:, :, pl.ds(8 * part, 8), :]
        a_ref[:, HALO + 8 : PLANES, 0, rows, :] = yh_ref[:, :, pl.ds(8 * part, 8), :]
        for c in range(3):
            right = xh_ref[3 * c + part]
            left = xl_ref[3 * c + part]
            for k in range(PLANES):
                a_ref[c, k, 1, rows, :] = jnp.where(
                    lane < 64,
                    pltpu.roll(right, (-HALO * k) % 128, 1),
                    pltpu.roll(left, (128 - HALO - HALO * k) % 128, 1),
                )

    gy = gy_ref[0]

    def close(ref):
        @pl.when(gy == 0)
        def _():
            ref[:, HALO - 1] = jnp.zeros((3, 2, 40, 128), jnp.float32)

        @pl.when(gy == last)
        def _():
            ref[:, HALO + 8] = jnp.zeros((3, 2, 40, 128), jnp.float32)

    def stage(source, target, combine, depth):
        @pl.loop(depth, PLANES - depth, unroll=2)
        def _(y):
            for row in (8, 16, 24):
                moved = _euler(source, y, row, 2)
                for c in range(3):
                    for t in range(2):
                        target[c, y, t, row : row + 8, :] = combine(moved[c][t], c, y, t, row)

        close(target)

    def keep(w, c, y, t, row):
        return w

    def quarter(w, c, y, t, row):
        return 0.75 * a_ref[c, y, t, row : row + 8, :] + 0.25 * w

    def third(w, c, y, t, row):
        return a_ref[c, y, t, row : row + 8, :] * (1.0 / 3.0) + (2.0 / 3.0) * w

    close(a_ref)
    stage(a_ref, b_ref, keep, 1)
    stage(b_ref, c_ref, quarter, 2)
    stage(c_ref, a_ref, third, 3)
    stage(a_ref, b_ref, keep, 4)
    stage(b_ref, c_ref, quarter, 5)
    for y in range(HALO, HALO + 8):
        moved = _euler(c_ref, y, 16, 1)
        for c in range(3):
            adv_ref[c, y - HALO] = third(moved[c][0], c, y, 0, 16)
    for c in range(3):
        for y in range(0, 8, 2):
            new_ref[c, y // 2] = adv_ref[c, y, pl.ds(0, 4, stride=2), :]


def near(x):
    return pltpu.with_memory_space_constraint(x, pltpu.VMEM)


VMEM_SPEC = pl.BlockSpec(memory_space=pltpu.VMEM)
SMEM_SPEC = pl.BlockSpec(memory_space=pltpu.SMEM)


def shift(x, axis, step):
    n = lax.axis_size(axis)
    return lax.ppermute(x, axis, [(i, (i + step) % n) for i in range(n)])


def advance(v):
    f32 = jnp.float32
    zl = shift(v, "gz", 1)
    zh = shift(v, "gz", -1)
    low, high = pl.pallas_call(
        _faces_y_kernel,
        out_shape=[pltpu.VMEM((3, HALO, 24, 128), f32)] * 2,
        in_specs=[VMEM_SPEC] * 3,
        out_specs=[VMEM_SPEC] * 2,
        name="faces_y",
    )(*map(near, (v, zl, zh)))
    yl = shift(high, "gy", 1)
    yh = shift(low, "gy", -1)
    low, high = pl.pallas_call(
        _faces_x_kernel,
        out_shape=[pltpu.VMEM((9, 8, 128), f32)] * 2,
        in_specs=[VMEM_SPEC] * 5,
        out_specs=[VMEM_SPEC] * 2,
        name="faces_x",
    )(*map(near, (v, zl, zh, yl, yh)))
    xl = shift(high, "grp", 1)
    xh = shift(low, "grp", -1)
    gy = lax.axis_index("gy").astype(jnp.int32).reshape(1)
    return pl.pallas_call(
        functools.partial(_stencil_kernel, last=lax.axis_size("gy") - 1),
        out_shape=[jax.ShapeDtypeStruct((3, 8, 8, 128), f32), pltpu.VMEM((3, 4, 4, 128), f32)],
        in_specs=[SMEM_SPEC] + [VMEM_SPEC] * 7,
        out_specs=[VMEM_SPEC] * 2,
        scratch_shapes=[pltpu.VMEM((3, PLANES, 2, 40, 128), f32)] * 3,
        name="stencil",
    )(gy, *map(near, (v, zl, zh, yl, yh, xh, xl)))


def exchanged(blocks, axes, groups):
    return lax.all_to_all(blocks, axes, 0, 0, axis_index_groups=groups)


def summed(gram):
    lanes = gram.shape[1]
    slow, mid, fast = (lax.axis_size(a) for a in ("grp", "gy", "gz"))
    parts, others = 2 * fast, slow * mid // 2
    rows = gram.shape[0] // parts
    near_groups = [[parts * i + j for j in range(parts)] for i in range(mid // 2)]
    far_groups = [[2 * i + core for i in range(others)] for core in range(2)]
    mine = jnp.sum(exchanged(gram.reshape(parts, rows, lanes), ("gy", "gz"), near_groups), axis=0)
    spread = jnp.broadcast_to(mine[None], (others, rows, lanes))
    mine = jnp.sum(exchanged(spread, ("grp", "gy"), far_groups), axis=0)
    spread = jnp.broadcast_to(mine[None], (parts, rows, lanes))
    return exchanged(spread, ("gy", "gz"), near_groups).reshape(gram.shape)


def _iterate_kernel(gram_ref, level_ref, weights_ref, *, total_rows):
    gram = gram_ref[...]
    scale = jnp.sqrt(jnp.sum(gram * gram, keepdims=True))
    level = gram / scale
    ident = (
        lax.broadcasted_iota(jnp.int32, (128, 128), 0) == lax.broadcasted_iota(jnp.int32, (128, 128), 1)
    ).astype(jnp.float32)

    def dot(a, b):
        return jnp.dot(a, b, precision=lax.Precision.HIGHEST, preferred_element_type=jnp.float32)

    inverse = ident
    for repeat in range(NS_ITERS):
        product = dot(inverse, level) if repeat else level
        factor = 1.5 * ident - 0.5 * product
        level = dot(level, factor)
        inverse = dot(factor, inverse) if repeat else factor
    level_ref[...] = level
    ratio = jnp.sqrt(jnp.float32(total_rows)) / jnp.sqrt(scale)
    weights_ref[...] = (inverse * ratio).astype(jnp.bfloat16)


def local(velocity, basis_old, strength, snapshots):
    modes = basis_old.shape[0]
    earlier_count = snapshots.shape[0]
    ranks = modes + earlier_count + 1
    head = (strength[:, None] * basis_old.reshape(modes, -1).astype(jnp.float32)).astype(jnp.bfloat16)
    field, newest = advance(velocity)
    newest = newest.reshape(1, -1).astype(jnp.bfloat16)
    whole = jnp.concatenate([head, snapshots.reshape(earlier_count, -1), newest], axis=0)
    gram = jnp.dot(whole, whole.T, preferred_element_type=jnp.float32)
    gram = summed(gram)
    total_rows = whole.shape[1] * lax.axis_size("grp") * lax.axis_size("gy") * lax.axis_size("gz")
    level, weights = pl.pallas_call(
        functools.partial(_iterate_kernel, total_rows=total_rows),
        out_shape=[
            jax.ShapeDtypeStruct((ranks, ranks), jnp.float32),
            pltpu.VMEM((ranks, ranks), jnp.bfloat16),
        ],
        in_specs=[VMEM_SPEC],
        out_specs=[VMEM_SPEC] * 2,
        name="iterate",
    )(near(gram))
    basis_new = jnp.dot(weights, whole, preferred_element_type=jnp.float32).astype(jnp.bfloat16)
    basis_new = basis_new.reshape(ranks, 3, field.shape[1] // 2, field.shape[2] // 2, field.shape[3])
    return (field, basis_new, level)


def solution(mesh):
    placed = (
        P(None, "gy", "gz", "grp"),
        P(None, None, "gy", "gz", "grp"),
        P(),
        P(None, None, "gy", "gz", "grp"),
    )
    return jax.shard_map(
        local,
        mesh=mesh,
        in_specs=placed,
        out_specs=(P(None, "gy", "gz", "grp"), P(None, None, "gy", "gz", "grp"), P()),
        check_vma=False,
    )
```

```python
import functools
import jax
import jax.numpy as jnp
from jax import lax
from jax.experimental import pallas as pl
from jax.experimental.pallas import tpu as pltpu
from jax.sharding import PartitionSpec as P

NS_ITERS = 8

HALO = 6
PLANES = 20
DT = 0.1
VISC = 0.05


def _lanes():
    return lax.broadcasted_iota(jnp.int32, (8, 128), 1)


def _faces_y_kernel(v_ref, zl_ref, zh_ref, low_ref, high_ref):
    for part, source in enumerate((zl_ref, v_ref, zh_ref)):
        rows = pl.ds(8 * part, 8)
        low_ref[:, :, rows, :] = source[:, 0:HALO]
        high_ref[:, :, rows, :] = source[:, 8 - HALO : 8]


def _plane(part, c, k, v_refs, yl_ref, yh_ref):
    rows = pl.ds(8 * part, 8)
    if k < HALO:
        return yl_ref[c, k, rows, :]
    if k < HALO + 8:
        return v_refs[part][c, k - HALO]
    return yh_ref[c, k - HALO - 8, rows, :]


def _faces_x_kernel(v_ref, zl_ref, zh_ref, yl_ref, yh_ref, low_ref, high_ref):
    lane = _lanes()
    sources = (zl_ref, v_ref, zh_ref)
    for c in range(3):
        for part in range(3):
            low = high = None
            for k in range(PLANES):
                tile = _plane(part, c, k, sources, yl_ref, yh_ref)
                first = pltpu.roll(tile, (HALO * k) % 128, 1)
                last = pltpu.roll(tile, (HALO * k + HALO) % 128, 1)
                if k == 0:
                    low, high = first, last
                else:
                    keep = lane < HALO * k
                    low = jnp.where(keep, low, first)
                    high = jnp.where(keep, high, last)
            low_ref[3 * c + part] = low
            high_ref[3 * c + part] = high


def _rotated(tiles, lane):
    up = [pltpu.roll(t, 127, 1) for t in tiles]
    down = [pltpu.roll(t, 1, 1) for t in tiles]
    plus = [jnp.where(lane == 127, up[1 - i], up[i]) for i in range(2)]
    minus = [jnp.where(lane == 0, down[1 - i], down[i]) for i in range(2)]
    return plus, minus


def _euler(u_ref, y, row, tiles):
    lane = _lanes()
    u = [[u_ref[c, y, t, row : row + 8, :] for t in range(2)] for c in range(3)]
    half = [[u[c][t] * (0.5 * DT) for t in range(tiles)] for c in range(3)]
    out = []
    for c in range(3):
        plus, minus = _rotated(u[c], lane)
        outs = []
        for t in range(tiles):
            yp = u_ref[c, y + 1, t, row : row + 8, :]
            ym = u_ref[c, y - 1, t, row : row + 8, :]
            zp = u_ref[c, y, t, row + 1 : row + 9, :]
            zm = u_ref[c, y, t, row - 1 : row + 7, :]
            carried = (
                half[0][t] * (plus[t] - minus[t])
                + half[1][t] * (yp - ym)
                + half[2][t] * (zp - zm)
            )
            around = (plus[t] + minus[t]) + (yp + ym) + (zp + zm)
            outs.append(u[c][t] + ((DT * VISC) * (around - 6.0 * u[c][t]) - carried))
        out.append(outs)
    return out


def _stencil_kernel(
    gy_ref, v_ref, zl_ref, zh_ref, yl_ref, yh_ref, xh_ref, xl_ref, adv_ref, new_ref, a_ref, b_ref, c_ref, *, last
):
    lane = _lanes()
    sources = (zl_ref, v_ref, zh_ref)
    for part in range(3):
        rows = pl.ds(8 + 8 * part, 8)
        a_ref[:, HALO : HALO + 8, 0, rows, :] = sources[part][...]
        a_ref[:, 0:HALO, 0, rows, :] = yl_ref[:, :, pl.ds(8 * part, 8), :]
        a_ref[:, HALO + 8 : PLANES, 0, rows, :] = yh_ref[:, :, pl.ds(8 * part, 8), :]
        for c in range(3):
            right = xh_ref[3 * c + part]
            left = xl_ref[3 * c + part]
            for k in range(PLANES):
                a_ref[c, k, 1, rows, :] = jnp.where(
                    lane < 64,
                    pltpu.roll(right, (-HALO * k) % 128, 1),
                    pltpu.roll(left, (128 - HALO - HALO * k) % 128, 1),
                )

    gy = gy_ref[0]

    def close(ref):
        @pl.when(gy == 0)
        def _():
            ref[:, HALO - 1] = jnp.zeros((3, 2, 40, 128), jnp.float32)

        @pl.when(gy == last)
        def _():
            ref[:, HALO + 8] = jnp.zeros((3, 2, 40, 128), jnp.float32)

    def stage(source, target, combine, depth):
        def plane(y, middle, outer):
            for row, tiles in ((8, outer), (16, middle), (24, outer)):
                if tiles:
                    moved = _euler(source, y, row, tiles)
                    for c in range(3):
                        for t in range(tiles):
                            target[c, y, t, row : row + 8, :] = combine(moved[c][t], c, y, t, row)

        plane(depth, 1, 0)
        plane(PLANES - 1 - depth, 1, 0)
        plane(depth + 1, 2, 1)
        plane(PLANES - 2 - depth, 2, 1)

        @pl.loop(depth + 2, PLANES - 2 - depth, unroll=2)
        def _(y):
            plane(y, 2, 2)

        close(target)

    def keep(w, c, y, t, row):
        return w

    def quarter(w, c, y, t, row):
        return 0.75 * a_ref[c, y, t, row : row + 8, :] + 0.25 * w

    def third(w, c, y, t, row):
        return a_ref[c, y, t, row : row + 8, :] * (1.0 / 3.0) + (2.0 / 3.0) * w

    close(a_ref)
    stage(a_ref, b_ref, keep, 1)
    stage(b_ref, c_ref, quarter, 2)
    stage(c_ref, a_ref, third, 3)
    stage(a_ref, b_ref, keep, 4)
    stage(b_ref, c_ref, quarter, 5)
    for y in range(HALO, HALO + 8):
        moved = _euler(c_ref, y, 16, 1)
        for c in range(3):
            adv_ref[c, y - HALO] = third(moved[c][0], c, y, 0, 16)
    for c in range(3):
        for y in range(0, 8, 2):
            new_ref[c, y // 2] = adv_ref[c, y, pl.ds(0, 4, stride=2), :]


def near(x):
    return pltpu.with_memory_space_constraint(x, pltpu.VMEM)


VMEM_SPEC = pl.BlockSpec(memory_space=pltpu.VMEM)
SMEM_SPEC = pl.BlockSpec(memory_space=pltpu.SMEM)


def shift(x, axis, step):
    n = lax.axis_size(axis)
    return lax.ppermute(x, axis, [(i, (i + step) % n) for i in range(n)])


def advance(v):
    f32 = jnp.float32
    zl = shift(v, "gz", 1)
    zh = shift(v, "gz", -1)
    v = jnp.where(lax.axis_index("gy") >= 0, v, 0.0)
    low, high = pl.pallas_call(
        _faces_y_kernel,
        out_shape=[pltpu.VMEM((3, HALO, 24, 128), f32)] * 2,
        in_specs=[VMEM_SPEC] * 3,
        out_specs=[VMEM_SPEC] * 2,
        name="faces_y",
    )(*map(near, (v, zl, zh)))
    yl = shift(high, "gy", 1)
    yh = shift(low, "gy", -1)
    low, high = pl.pallas_call(
        _faces_x_kernel,
        out_shape=[pltpu.VMEM((9, 8, 128), f32)] * 2,
        in_specs=[VMEM_SPEC] * 5,
        out_specs=[VMEM_SPEC] * 2,
        name="faces_x",
    )(*map(near, (v, zl, zh, yl, yh)))
    xl = shift(high, "grp", 1)
    xh = shift(low, "grp", -1)
    gy = lax.axis_index("gy").astype(jnp.int32).reshape(1)
    return pl.pallas_call(
        functools.partial(_stencil_kernel, last=lax.axis_size("gy") - 1),
        out_shape=[jax.ShapeDtypeStruct((3, 8, 8, 128), f32), pltpu.VMEM((3, 4, 4, 128), f32)],
        in_specs=[SMEM_SPEC] + [VMEM_SPEC] * 7,
        out_specs=[VMEM_SPEC] * 2,
        scratch_shapes=[pltpu.VMEM((3, PLANES, 2, 40, 128), f32)] * 3,
        name="stencil",
    )(gy, *map(near, (v, zl, zh, yl, yh, xh, xl)))


def exchanged(blocks, axes, groups):
    return lax.all_to_all(blocks, axes, 0, 0, axis_index_groups=groups)


def summed(gram):
    lanes = gram.shape[1]
    slow, mid, fast = (lax.axis_size(a) for a in ("grp", "gy", "gz"))
    parts, others = 2 * fast, slow * mid // 2
    rows = gram.shape[0] // parts
    near_groups = [[parts * i + j for j in range(parts)] for i in range(mid // 2)]
    far_groups = [[2 * i + core for i in range(others)] for core in range(2)]
    mine = jnp.sum(exchanged(gram.reshape(parts, rows, lanes), ("gy", "gz"), near_groups), axis=0)
    spread = jnp.broadcast_to(mine[None], (others, rows, lanes))
    mine = jnp.sum(exchanged(spread, ("grp", "gy"), far_groups), axis=0)
    spread = jnp.broadcast_to(mine[None], (parts, rows, lanes))
    return exchanged(spread, ("gy", "gz"), near_groups).reshape(gram.shape)


def _iterate_kernel(gram_ref, level_ref, weights_ref, *, total_rows):
    gram = gram_ref[...]
    scale = jnp.sqrt(jnp.sum(gram * gram, keepdims=True))
    level = gram / scale
    ident = (
        lax.broadcasted_iota(jnp.int32, (128, 128), 0) == lax.broadcasted_iota(jnp.int32, (128, 128), 1)
    ).astype(jnp.float32)

    def dot(a, b):
        return jnp.dot(a, b, precision=lax.Precision.HIGHEST, preferred_element_type=jnp.float32)

    inverse = ident
    for repeat in range(NS_ITERS):
        product = dot(inverse, level) if repeat else level
        factor = 1.5 * ident - 0.5 * product
        level = dot(level, factor)
        inverse = dot(factor, inverse) if repeat else factor
    level_ref[...] = level
    ratio = jnp.sqrt(jnp.float32(total_rows)) / jnp.sqrt(scale)
    weights_ref[...] = (inverse * ratio).astype(jnp.bfloat16)


def local(velocity, basis_old, strength, snapshots):
    modes = basis_old.shape[0]
    earlier_count = snapshots.shape[0]
    ranks = modes + earlier_count + 1
    head = (strength[:, None] * basis_old.reshape(modes, -1).astype(jnp.float32)).astype(jnp.bfloat16)
    field, newest = advance(velocity)
    newest = newest.reshape(1, -1).astype(jnp.bfloat16)
    whole = jnp.concatenate([head, snapshots.reshape(earlier_count, -1), newest], axis=0)
    gram = jnp.dot(whole, whole.T, preferred_element_type=jnp.float32)
    gram = summed(gram)
    total_rows = whole.shape[1] * lax.axis_size("grp") * lax.axis_size("gy") * lax.axis_size("gz")
    level, weights = pl.pallas_call(
        functools.partial(_iterate_kernel, total_rows=total_rows),
        out_shape=[
            jax.ShapeDtypeStruct((ranks, ranks), jnp.float32),
            pltpu.VMEM((ranks, ranks), jnp.bfloat16),
        ],
        in_specs=[VMEM_SPEC],
        out_specs=[VMEM_SPEC] * 2,
        name="iterate",
    )(near(gram))
    basis_new = jnp.dot(weights, whole, preferred_element_type=jnp.float32).astype(jnp.bfloat16)
    basis_new = basis_new.reshape(ranks, 3, field.shape[1] // 2, field.shape[2] // 2, field.shape[3])
    return (field, basis_new, level)


def solution(mesh):
    placed = (
        P(None, "gy", "gz", "grp"),
        P(None, None, "gy", "gz", "grp"),
        P(),
        P(None, None, "gy", "gz", "grp"),
    )
    return jax.shard_map(
        local,
        mesh=mesh,
        in_specs=placed,
        out_specs=(P(None, "gy", "gz", "grp"), P(None, None, "gy", "gz", "grp"), P()),
        check_vma=False,
    )
```

```python
import functools
import jax
import jax.numpy as jnp
from jax import lax
from jax.experimental import pallas as pl
from jax.experimental.pallas import tpu as pltpu
from jax.sharding import PartitionSpec as P

NS_ITERS = 8

HALO = 6
PLANES = 20
DT = 0.1
VISC = 0.05


def _lanes():
    return lax.broadcasted_iota(jnp.int32, (8, 128), 1)


def _faces_y_kernel(v_ref, zl_ref, zh_ref, low_ref, high_ref):
    for part, source in enumerate((zl_ref, v_ref, zh_ref)):
        rows = pl.ds(8 * part, 8)
        low_ref[:, :, rows, :] = source[:, 0:HALO]
        high_ref[:, :, rows, :] = source[:, 8 - HALO : 8]


def _plane(part, c, k, v_refs, yl_ref, yh_ref):
    rows = pl.ds(8 * part, 8)
    if k < HALO:
        return yl_ref[c, k, rows, :]
    if k < HALO + 8:
        return v_refs[part][c, k - HALO]
    return yh_ref[c, k - HALO - 8, rows, :]


def _faces_x_kernel(v_ref, zl_ref, zh_ref, yl_ref, yh_ref, low_ref, high_ref):
    lane = _lanes()
    sources = (zl_ref, v_ref, zh_ref)
    for c in range(3):
        for part in range(3):
            low = high = None
            for k in range(PLANES):
                tile = _plane(part, c, k, sources, yl_ref, yh_ref)
                first = pltpu.roll(tile, (HALO * k) % 128, 1)
                last = pltpu.roll(tile, (HALO * k + HALO) % 128, 1)
                if k == 0:
                    low, high = first, last
                else:
                    keep = lane < HALO * k
                    low = jnp.where(keep, low, first)
                    high = jnp.where(keep, high, last)
            low_ref[3 * c + part] = low
            high_ref[3 * c + part] = high


def _rotated(tiles, lane):
    up = [pltpu.roll(t, 127, 1) for t in tiles]
    down = [pltpu.roll(t, 1, 1) for t in tiles]
    plus = [jnp.where(lane == 127, up[1 - i], up[i]) for i in range(2)]
    minus = [jnp.where(lane == 0, down[1 - i], down[i]) for i in range(2)]
    return plus, minus


def _euler(u_ref, y, row, tiles, share):
    lane = _lanes()
    spread = share * DT * VISC
    u = [[u_ref[c, y, t, row : row + 8, :] for t in range(2)] for c in range(3)]
    half = [[u[c][t] * (share * 0.5 * DT) for t in range(tiles)] for c in range(3)]
    ahead = [[spread - half[c][t] for t in range(tiles)] for c in range(3)]
    behind = [[spread + half[c][t] for t in range(tiles)] for c in range(3)]
    out = []
    for c in range(3):
        plus, minus = _rotated(u[c], lane)
        outs = []
        for t in range(tiles):
            yp = u_ref[c, y + 1, t, row : row + 8, :]
            ym = u_ref[c, y - 1, t, row : row + 8, :]
            zp = u_ref[c, y, t, row + 1 : row + 9, :]
            zm = u_ref[c, y, t, row - 1 : row + 7, :]
            outs.append(
                (u[c][t] * (share - 6.0 * spread) + (plus[t] * ahead[0][t] + minus[t] * behind[0][t]))
                + ((yp * ahead[1][t] + ym * behind[1][t]) + (zp * ahead[2][t] + zm * behind[2][t]))
            )
        out.append(outs)
    return out


def _stencil_kernel(
    gy_ref, v_ref, zl_ref, zh_ref, yl_ref, yh_ref, xh_ref, xl_ref, adv_ref, new_ref, a_ref, b_ref, c_ref, *, last
):
    lane = _lanes()
    sources = (zl_ref, v_ref, zh_ref)
    for part in range(3):
        rows = pl.ds(8 + 8 * part, 8)
        a_ref[:, HALO : HALO + 8, 0, rows, :] = sources[part][...]
        a_ref[:, 0:HALO, 0, rows, :] = yl_ref[:, :, pl.ds(8 * part, 8), :]
        a_ref[:, HALO + 8 : PLANES, 0, rows, :] = yh_ref[:, :, pl.ds(8 * part, 8), :]
        for c in range(3):
            right = xh_ref[3 * c + part]
            left = xl_ref[3 * c + part]
            for k in range(PLANES):
                a_ref[c, k, 1, rows, :] = jnp.where(
                    lane < 64,
                    pltpu.roll(right, (-HALO * k) % 128, 1),
                    pltpu.roll(left, (128 - HALO - HALO * k) % 128, 1),
                )

    gy = gy_ref[0]

    def close(ref):
        @pl.when(gy == 0)
        def _():
            ref[:, HALO - 1] = jnp.zeros((3, 2, 40, 128), jnp.float32)

        @pl.when(gy == last)
        def _():
            ref[:, HALO + 8] = jnp.zeros((3, 2, 40, 128), jnp.float32)

    def stage(source, target, own, share, depth):
        def plane(y, middle, outer):
            for row, tiles in ((8, outer), (16, middle), (24, outer)):
                if tiles:
                    moved = _euler(source, y, row, tiles, share)
                    for c in range(3):
                        for t in range(tiles):
                            value = moved[c][t]
                            if own:
                                value = value + own * a_ref[c, y, t, row : row + 8, :]
                            target[c, y, t, row : row + 8, :] = value

        plane(depth, 1, 0)
        plane(PLANES - 1 - depth, 1, 0)
        plane(depth + 1, 2, 1)
        plane(PLANES - 2 - depth, 2, 1)

        @pl.loop(depth + 2, PLANES - 2 - depth, unroll=2)
        def _(y):
            plane(y, 2, 2)

        close(target)

    close(a_ref)
    stage(a_ref, b_ref, 0.0, 1.0, 1)
    stage(b_ref, c_ref, 0.75, 0.25, 2)
    stage(c_ref, a_ref, 1.0 / 3.0, 2.0 / 3.0, 3)
    stage(a_ref, b_ref, 0.0, 1.0, 4)
    stage(b_ref, c_ref, 0.75, 0.25, 5)
    for y in range(HALO, HALO + 8):
        moved = _euler(c_ref, y, 16, 1, 2.0 / 3.0)
        for c in range(3):
            adv_ref[c, y - HALO] = moved[c][0] + a_ref[c, y, 0, 16:24, :] * (1.0 / 3.0)
    for c in range(3):
        for y in range(0, 8, 2):
            new_ref[c, y // 2] = adv_ref[c, y, pl.ds(0, 4, stride=2), :]


def near(x):
    return pltpu.with_memory_space_constraint(x, pltpu.VMEM)


VMEM_SPEC = pl.BlockSpec(memory_space=pltpu.VMEM)
SMEM_SPEC = pl.BlockSpec(memory_space=pltpu.SMEM)


def shift(x, axis, step):
    n = lax.axis_size(axis)
    return lax.ppermute(x, axis, [(i, (i + step) % n) for i in range(n)])


def advance(v):
    f32 = jnp.float32
    zl = shift(v, "gz", 1)
    zh = shift(v, "gz", -1)
    v = jnp.where(lax.axis_index("gy") >= 0, v, 0.0)
    low, high = pl.pallas_call(
        _faces_y_kernel,
        out_shape=[pltpu.VMEM((3, HALO, 24, 128), f32)] * 2,
        in_specs=[VMEM_SPEC] * 3,
        out_specs=[VMEM_SPEC] * 2,
        name="faces_y",
    )(*map(near, (v, zl, zh)))
    yl = shift(high, "gy", 1)
    yh = shift(low, "gy", -1)
    low, high = pl.pallas_call(
        _faces_x_kernel,
        out_shape=[pltpu.VMEM((9, 8, 128), f32)] * 2,
        in_specs=[VMEM_SPEC] * 5,
        out_specs=[VMEM_SPEC] * 2,
        name="faces_x",
    )(*map(near, (v, zl, zh, yl, yh)))
    xl = shift(high, "grp", 1)
    xh = shift(low, "grp", -1)
    gy = lax.axis_index("gy").astype(jnp.int32).reshape(1)
    return pl.pallas_call(
        functools.partial(_stencil_kernel, last=lax.axis_size("gy") - 1),
        out_shape=[jax.ShapeDtypeStruct((3, 8, 8, 128), f32), pltpu.VMEM((3, 4, 4, 128), f32)],
        in_specs=[SMEM_SPEC] + [VMEM_SPEC] * 7,
        out_specs=[VMEM_SPEC] * 2,
        scratch_shapes=[pltpu.VMEM((3, PLANES, 2, 40, 128), f32)] * 3,
        name="stencil",
    )(gy, *map(near, (v, zl, zh, yl, yh, xh, xl)))


def exchanged(blocks, axes, groups):
    return lax.all_to_all(blocks, axes, 0, 0, axis_index_groups=groups)


def summed(gram):
    lanes = gram.shape[1]
    slow, mid, fast = (lax.axis_size(a) for a in ("grp", "gy", "gz"))
    parts, others = 2 * fast, slow * mid // 2
    rows = gram.shape[0] // parts
    near_groups = [[parts * i + j for j in range(parts)] for i in range(mid // 2)]
    far_groups = [[2 * i + core for i in range(others)] for core in range(2)]
    mine = jnp.sum(exchanged(gram.reshape(parts, rows, lanes), ("gy", "gz"), near_groups), axis=0)
    spread = jnp.broadcast_to(mine[None], (others, rows, lanes))
    mine = jnp.sum(exchanged(spread, ("grp", "gy"), far_groups), axis=0)
    spread = jnp.broadcast_to(mine[None], (parts, rows, lanes))
    return exchanged(spread, ("gy", "gz"), near_groups).reshape(gram.shape)


def _iterate_kernel(gram_ref, level_ref, weights_ref, *, total_rows):
    gram = gram_ref[...]
    scale = jnp.sqrt(jnp.sum(gram * gram, keepdims=True))
    level = gram / scale
    ident = (
        lax.broadcasted_iota(jnp.int32, (128, 128), 0) == lax.broadcasted_iota(jnp.int32, (128, 128), 1)
    ).astype(jnp.float32)

    def dot(a, b):
        return jnp.dot(a, b, precision=lax.Precision.HIGHEST, preferred_element_type=jnp.float32)

    inverse = ident
    for repeat in range(NS_ITERS):
        product = dot(inverse, level) if repeat else level
        factor = 1.5 * ident - 0.5 * product
        level = dot(level, factor)
        inverse = dot(factor, inverse) if repeat else factor
    level_ref[...] = level
    ratio = jnp.sqrt(jnp.float32(total_rows)) / jnp.sqrt(scale)
    weights_ref[...] = (inverse * ratio).astype(jnp.bfloat16)


def local(velocity, basis_old, strength, snapshots):
    modes = basis_old.shape[0]
    earlier_count = snapshots.shape[0]
    ranks = modes + earlier_count + 1
    head = (strength[:, None] * basis_old.reshape(modes, -1).astype(jnp.float32)).astype(jnp.bfloat16)
    field, newest = advance(velocity)
    newest = newest.reshape(1, -1).astype(jnp.bfloat16)
    whole = jnp.concatenate([head, snapshots.reshape(earlier_count, -1), newest], axis=0)
    gram = jnp.dot(whole, whole.T, preferred_element_type=jnp.float32)
    gram = summed(gram)
    total_rows = whole.shape[1] * lax.axis_size("grp") * lax.axis_size("gy") * lax.axis_size("gz")
    level, weights = pl.pallas_call(
        functools.partial(_iterate_kernel, total_rows=total_rows),
        out_shape=[
            jax.ShapeDtypeStruct((ranks, ranks), jnp.float32),
            pltpu.VMEM((ranks, ranks), jnp.bfloat16),
        ],
        in_specs=[VMEM_SPEC],
        out_specs=[VMEM_SPEC] * 2,
        name="iterate",
    )(near(gram))
    basis_new = jnp.dot(weights, whole, preferred_element_type=jnp.float32).astype(jnp.bfloat16)
    basis_new = basis_new.reshape(ranks, 3, field.shape[1] // 2, field.shape[2] // 2, field.shape[3])
    return (field, basis_new, level)


def solution(mesh):
    placed = (
        P(None, "gy", "gz", "grp"),
        P(None, None, "gy", "gz", "grp"),
        P(),
        P(None, None, "gy", "gz", "grp"),
    )
    return jax.shard_map(
        local,
        mesh=mesh,
        in_specs=placed,
        out_specs=(P(None, "gy", "gz", "grp"), P(None, None, "gy", "gz", "grp"), P()),
        check_vma=False,
    )
```

```python
import functools
import jax
import jax.numpy as jnp
from jax import lax
from jax.experimental import pallas as pl
from jax.experimental.pallas import tpu as pltpu
from jax.sharding import PartitionSpec as P

NS_ITERS = 8

HALO = 6
PLANES = 20
DT = 0.1
VISC = 0.05


def _lanes():
    return lax.broadcasted_iota(jnp.int32, (8, 128), 1)


def _faces_y_kernel(v_ref, zl_ref, zh_ref, low_ref, high_ref):
    for part, source in enumerate((zl_ref, v_ref, zh_ref)):
        rows = pl.ds(8 * part, 8)
        low_ref[:, :, rows, :] = source[:, 0:HALO]
        high_ref[:, :, rows, :] = source[:, 8 - HALO : 8]


def _plane(part, c, k, v_refs, yl_ref, yh_ref):
    rows = pl.ds(8 * part, 8)
    if k < HALO:
        return yl_ref[c, k, rows, :]
    if k < HALO + 8:
        return v_refs[part][c, k - HALO]
    return yh_ref[c, k - HALO - 8, rows, :]


def _faces_x_kernel(v_ref, zl_ref, zh_ref, yl_ref, yh_ref, low_ref, high_ref):
    lane = _lanes()
    sources = (zl_ref, v_ref, zh_ref)
    for c in range(3):
        for part in range(3):
            low = high = None
            for k in range(PLANES):
                tile = _plane(part, c, k, sources, yl_ref, yh_ref)
                first = pltpu.roll(tile, (HALO * k) % 128, 1)
                last = pltpu.roll(tile, (HALO * k + HALO) % 128, 1)
                if k == 0:
                    low, high = first, last
                else:
                    keep = lane < HALO * k
                    low = jnp.where(keep, low, first)
                    high = jnp.where(keep, high, last)
            low_ref[3 * c + part] = low
            high_ref[3 * c + part] = high


def _rotated(tiles, lane):
    up = [pltpu.roll(t, 127, 1) for t in tiles]
    down = [pltpu.roll(t, 1, 1) for t in tiles]
    plus = [jnp.where(lane == 127, up[1 - i], up[i]) for i in range(2)]
    minus = [jnp.where(lane == 0, down[1 - i], down[i]) for i in range(2)]
    return plus, minus


def _euler(u_ref, y, row, tiles, share):
    lane = _lanes()
    spread = share * DT * VISC
    u = [[u_ref[c, y, t, row : row + 8, :] for t in range(2)] for c in range(3)]
    half = [[u[c][t] * (share * 0.5 * DT) for t in range(tiles)] for c in range(3)]
    ahead = [[spread - half[c][t] for t in range(tiles)] for c in range(3)]
    behind = [[spread + half[c][t] for t in range(tiles)] for c in range(3)]
    out = []
    for c in range(3):
        plus, minus = _rotated(u[c], lane)
        outs = []
        for t in range(tiles):
            yp = u_ref[c, y + 1, t, row : row + 8, :]
            ym = u_ref[c, y - 1, t, row : row + 8, :]
            zp = u_ref[c, y, t, row + 1 : row + 9, :]
            zm = u_ref[c, y, t, row - 1 : row + 7, :]
            outs.append(
                (u[c][t] * (share - 6.0 * spread) + (plus[t] * ahead[0][t] + minus[t] * behind[0][t]))
                + ((yp * ahead[1][t] + ym * behind[1][t]) + (zp * ahead[2][t] + zm * behind[2][t]))
            )
        out.append(outs)
    return out


def _stencil_kernel(
    gy_ref, v_ref, zl_ref, zh_ref, yl_ref, yh_ref, xh_ref, xl_ref, adv_ref, new_ref, a_ref, b_ref, c_ref, *, last
):
    lane = _lanes()
    sources = (zl_ref, v_ref, zh_ref)
    for part in range(3):
        rows = pl.ds(8 + 8 * part, 8)
        a_ref[:, HALO : HALO + 8, 0, rows, :] = sources[part][...]
        a_ref[:, 0:HALO, 0, rows, :] = yl_ref[:, :, pl.ds(8 * part, 8), :]
        a_ref[:, HALO + 8 : PLANES, 0, rows, :] = yh_ref[:, :, pl.ds(8 * part, 8), :]
        for c in range(3):
            right = xh_ref[3 * c + part]
            left = xl_ref[3 * c + part]
            for k in range(PLANES):
                a_ref[c, k, 1, rows, :] = jnp.where(
                    lane < 64,
                    pltpu.roll(right, (-HALO * k) % 128, 1),
                    pltpu.roll(left, (128 - HALO - HALO * k) % 128, 1),
                )

    gy = gy_ref[0]

    def close(ref):
        @pl.when(gy == 0)
        def _():
            ref[:, HALO - 1] = jnp.zeros((3, 2, 40, 128), jnp.float32)

        @pl.when(gy == last)
        def _():
            ref[:, HALO + 8] = jnp.zeros((3, 2, 40, 128), jnp.float32)

    def stage(source, target, own, share, depth):
        def plane(y, middle, outer):
            for row, tiles in ((8, outer), (16, middle), (24, outer)):
                if tiles:
                    moved = _euler(source, y, row, tiles, share)
                    for c in range(3):
                        for t in range(tiles):
                            value = moved[c][t]
                            if own:
                                value = value + own * a_ref[c, y, t, row : row + 8, :]
                            target[c, y, t, row : row + 8, :] = value

        plane(depth, 1, 0)
        plane(PLANES - 1 - depth, 1, 0)
        plane(depth + 1, 2, 1)
        plane(PLANES - 2 - depth, 2, 1)

        for y in range(depth + 2, PLANES - 2 - depth):
            plane(y, 2, 2)

        close(target)

    close(a_ref)
    stage(a_ref, b_ref, 0.0, 1.0, 1)
    stage(b_ref, c_ref, 0.75, 0.25, 2)
    stage(c_ref, a_ref, 1.0 / 3.0, 2.0 / 3.0, 3)
    stage(a_ref, b_ref, 0.0, 1.0, 4)
    stage(b_ref, c_ref, 0.75, 0.25, 5)
    for y in range(HALO, HALO + 8):
        moved = _euler(c_ref, y, 16, 1, 2.0 / 3.0)
        for c in range(3):
            adv_ref[c, y - HALO] = moved[c][0] + a_ref[c, y, 0, 16:24, :] * (1.0 / 3.0)
    for c in range(3):
        for y in range(0, 8, 2):
            new_ref[c, y // 2] = adv_ref[c, y, pl.ds(0, 4, stride=2), :]


def near(x):
    return pltpu.with_memory_space_constraint(x, pltpu.VMEM)


VMEM_SPEC = pl.BlockSpec(memory_space=pltpu.VMEM)
SMEM_SPEC = pl.BlockSpec(memory_space=pltpu.SMEM)


def shift(x, axis, step):
    n = lax.axis_size(axis)
    return lax.ppermute(x, axis, [(i, (i + step) % n) for i in range(n)])


def advance(v):
    f32 = jnp.float32
    zl = shift(v, "gz", 1)
    zh = shift(v, "gz", -1)
    v = jnp.where(lax.axis_index("gy") >= 0, v, 0.0)
    low, high = pl.pallas_call(
        _faces_y_kernel,
        out_shape=[pltpu.VMEM((3, HALO, 24, 128), f32)] * 2,
        in_specs=[VMEM_SPEC] * 3,
        out_specs=[VMEM_SPEC] * 2,
        name="faces_y",
    )(*map(near, (v, zl, zh)))
    yl = shift(high, "gy", 1)
    yh = shift(low, "gy", -1)
    low, high = pl.pallas_call(
        _faces_x_kernel,
        out_shape=[pltpu.VMEM((9, 8, 128), f32)] * 2,
        in_specs=[VMEM_SPEC] * 5,
        out_specs=[VMEM_SPEC] * 2,
        name="faces_x",
    )(*map(near, (v, zl, zh, yl, yh)))
    xl = shift(high, "grp", 1)
    xh = shift(low, "grp", -1)
    gy = lax.axis_index("gy").astype(jnp.int32).reshape(1)
    return pl.pallas_call(
        functools.partial(_stencil_kernel, last=lax.axis_size("gy") - 1),
        out_shape=[jax.ShapeDtypeStruct((3, 8, 8, 128), f32), pltpu.VMEM((3, 4, 4, 128), f32)],
        in_specs=[SMEM_SPEC] + [VMEM_SPEC] * 7,
        out_specs=[VMEM_SPEC] * 2,
        scratch_shapes=[pltpu.VMEM((3, PLANES, 2, 40, 128), f32)] * 3,
        name="stencil",
    )(gy, *map(near, (v, zl, zh, yl, yh, xh, xl)))


def exchanged(blocks, axes, groups):
    return lax.all_to_all(blocks, axes, 0, 0, axis_index_groups=groups)


def summed(gram):
    lanes = gram.shape[1]
    slow, mid, fast = (lax.axis_size(a) for a in ("grp", "gy", "gz"))
    parts, others = 2 * fast, slow * mid // 2
    rows = gram.shape[0] // parts
    near_groups = [[parts * i + j for j in range(parts)] for i in range(mid // 2)]
    far_groups = [[2 * i + core for i in range(others)] for core in range(2)]
    mine = jnp.sum(exchanged(gram.reshape(parts, rows, lanes), ("gy", "gz"), near_groups), axis=0)
    spread = jnp.broadcast_to(mine[None], (others, rows, lanes))
    mine = jnp.sum(exchanged(spread, ("grp", "gy"), far_groups), axis=0)
    spread = jnp.broadcast_to(mine[None], (parts, rows, lanes))
    return exchanged(spread, ("gy", "gz"), near_groups).reshape(gram.shape)


def _iterate_kernel(gram_ref, level_ref, weights_ref, *, total_rows):
    gram = gram_ref[...]
    scale = jnp.sqrt(jnp.sum(gram * gram, keepdims=True))
    level = gram / scale
    ident = (
        lax.broadcasted_iota(jnp.int32, (128, 128), 0) == lax.broadcasted_iota(jnp.int32, (128, 128), 1)
    ).astype(jnp.float32)

    def dot(a, b):
        return jnp.dot(a, b, precision=lax.Precision.HIGHEST, preferred_element_type=jnp.float32)

    inverse = ident
    for repeat in range(NS_ITERS):
        product = dot(inverse, level) if repeat else level
        factor = 1.5 * ident - 0.5 * product
        level = dot(level, factor)
        inverse = dot(factor, inverse) if repeat else factor
    level_ref[...] = level
    ratio = jnp.sqrt(jnp.float32(total_rows)) / jnp.sqrt(scale)
    weights_ref[...] = (inverse * ratio).astype(jnp.bfloat16)


def local(velocity, basis_old, strength, snapshots):
    modes = basis_old.shape[0]
    earlier_count = snapshots.shape[0]
    ranks = modes + earlier_count + 1
    head = (strength[:, None] * basis_old.reshape(modes, -1).astype(jnp.float32)).astype(jnp.bfloat16)
    field, newest = advance(velocity)
    newest = newest.reshape(1, -1).astype(jnp.bfloat16)
    whole = jnp.concatenate([head, snapshots.reshape(earlier_count, -1), newest], axis=0)
    gram = jnp.dot(whole, whole.T, preferred_element_type=jnp.float32)
    gram = summed(gram)
    total_rows = whole.shape[1] * lax.axis_size("grp") * lax.axis_size("gy") * lax.axis_size("gz")
    level, weights = pl.pallas_call(
        functools.partial(_iterate_kernel, total_rows=total_rows),
        out_shape=[
            jax.ShapeDtypeStruct((ranks, ranks), jnp.float32),
            pltpu.VMEM((ranks, ranks), jnp.bfloat16),
        ],
        in_specs=[VMEM_SPEC],
        out_specs=[VMEM_SPEC] * 2,
        name="iterate",
    )(near(gram))
    basis_new = jnp.dot(weights, whole, preferred_element_type=jnp.float32).astype(jnp.bfloat16)
    basis_new = basis_new.reshape(ranks, 3, field.shape[1] // 2, field.shape[2] // 2, field.shape[3])
    return (field, basis_new, level)


def solution(mesh):
    placed = (
        P(None, "gy", "gz", "grp"),
        P(None, None, "gy", "gz", "grp"),
        P(),
        P(None, None, "gy", "gz", "grp"),
    )
    return jax.shard_map(
        local,
        mesh=mesh,
        in_specs=placed,
        out_specs=(P(None, "gy", "gz", "grp"), P(None, None, "gy", "gz", "grp"), P()),
        check_vma=False,
    )
```
